32 devices in a mesh: dp: 4 (over x, core), enc: 8 (over z, y).
Axes of the slice: x: 2, y: 2, z: 4, core: 2. Of those that a mesh axis runs over, the one named last changes fastest.
Arguments:
- hidden_states: bfloat16 [2048, 4096], P('dp', 'enc'), as said below
- dec_gain: bfloat16 [4096], replicated, as said below
- nbr_tokens: bfloat16 [48, 128, 4096], P('dp', 'enc'), as said below
- enc_gain: bfloat16 [4096], replicated, as said below
- query_weight: bfloat16 [4096, 4096], P(None, 'enc'), may hold values from -0.09375 to 0.09375
- key_weight: bfloat16 [4096, 4096], P(None, 'enc'), may hold values from -0.09375 to 0.09375
- value_weight: bfloat16 [4096, 4096], P(None, 'enc'), may hold values from -0.09375 to 0.09375
- out_weight: bfloat16 [4096, 4096], P('enc'), may hold values from -0.09375 to 0.09375
- cite_owner: int32 [64, 1], P('dp'), may hold values from 0 to 3; in each aligned block of 16 rows (0 to 15, 16 to 31, ...) at most 8 rows name the same one
- cite_local: int32 [32, 2], P('dp'), may hold values from 0 to 11
Outputs:
- block_out: bfloat16 [2048, 4096], P(('dp', 'enc'))
The draws below stay inside these ranges and needn't reach their ends.
Inputs may be any that keep to these rules, and one draw needn't show every extreme that they name: `cite_owner`: among the citations of one index of dp, no owner is named more than 8 times, a bound that some block reaches. `hidden_states`: token rows have widely differing magnitudes. `nbr_tokens`: token rows have widely differing magnitudes. `dec_gain`: Positive. `enc_gain`: Positive.
All inputs are finite; a program needn't handle non-finite values.
Results may differ from the reference program's by a relative error of at most 0.013.
The reference program's roundings to bfloat16 on the way count: a program that leaves them out, or rounds other values in their place, can miss the bound.
Values may be sent and summed in bfloat16 or wider, within the bound.
A program may use at most 128 MiB of HBM per device.

```python
import math
import jax
import jax.numpy as jnp
import numpy as np
from jax import lax

D = 4096
H = 32
HD = 128
SPAN = 64
NL = 128
NBRS = 2
CH_DEV = 8
NU_DEV = 12
CAP = 8
SPANS = 32
TOKENS = 2048
NU = 48
N_DP = 4
N_ENC = 8


def rough_rows(key, shape):
    base_key, scale_key = jax.random.split(key, 2)
    row_shape = shape[:-1] + (1,)
    scales = jnp.exp(jax.random.uniform(scale_key, row_shape, jnp.float32, 0.0, math.log(10.0)))
    base = jnp.clip(jax.random.normal(base_key, shape, jnp.float32), -5.0, 5.0)
    return (scales * base).astype(jnp.bfloat16)


def gain_values(key):
    return jnp.clip(1.0 + 0.3 * jax.random.normal(key, (D,), jnp.float32), 0.3, 1.7)


def draw_hidden_states(key, part):
    return rough_rows(jax.random.fold_in(key, 11), (TOKENS, D))


def draw_nbr_tokens(key, part):
    return rough_rows(jax.random.fold_in(key, 23), (NU, NL, D))


def draw_dec_gain(key, part):
    return gain_values(jax.random.fold_in(key, 37)).astype(jnp.bfloat16)


def draw_enc_gain(key, part):
    return gain_values(jax.random.fold_in(key, 41)).astype(jnp.bfloat16)


def set_ends(array, own_key, smallest, largest):
    longest = array.shape.index(max(array.shape))
    spots = []
    for shift in (0, 1):
        where = [jax.random.randint(jax.random.fold_in(own_key, axis), (), 0, length) for axis, length in enumerate(array.shape)]
        where[longest] = (where[longest] + shift) % array.shape[longest]
        spots.append(tuple(where))
    return array.at[spots[0]].set(smallest).at[spots[1]].set(largest)


def shard_levels(rng, dims, shards, least, top_value):
    loudness, own = 1.0, jax.random.fold_in(rng, 6)
    for dim, shards_of in shards:
        draws = jnp.exp(jax.random.uniform(jax.random.fold_in(own, dim), (shards_of,), jnp.float32, least / len(shards), top_value / len(shards)))
        loudness = loudness * jnp.repeat(draws, dims[dim] // shards_of).reshape([-1 if axis == dim else 1 for axis in range(len(dims))])
    return loudness


def deal_out(own_key, own, number, rows, count, top, limit, lean):
    order = jax.random.permutation(own_key, count)
    heavy_load, usual = portions_of(count, rows * top, limit, lean, True), portions_of(count, rows * top, limit, lean, False)
    places = jnp.arange(count)

    def named(tallies, turn):
        used = int((tallies > 0).sum())
        fixed = max(1, used // 4)
        shifted = fixed + (places - fixed + turn * (used - fixed)) % max(1, count - fixed)
        return jnp.zeros((count,), jnp.int32).at[order[jnp.where(places < fixed, places, shifted)]].set(jnp.asarray(tallies, jnp.int32))

    tallies = jnp.where(number % 4 == 0, named(heavy_load, number // 4), named(usual, number - number // 4 - 1))
    mixed = jax.random.permutation(jax.random.fold_in(own, 3), count)
    donor, receiver = mixed[0:count // 2 * 2:2], mixed[1:count // 2 * 2:2]
    room = jnp.minimum(tallies[donor] - 1, limit - tallies[receiver]) // 2
    room = jnp.where((donor == order[0]) | (receiver == order[0]) | (tallies[receiver] == 0), 0, jnp.maximum(room, 0))
    shifted = jax.random.randint(jax.random.fold_in(own, 4), (count // 2,), 0, 1 << 20) % (room + 1)
    tallies = tallies.at[donor].add(-shifted).at[receiver].add(shifted)
    members = jnp.searchsorted(jnp.cumsum(tallies), jnp.arange(rows * top), side="right").astype(jnp.int32)
    listing = members.reshape(top, rows).T
    listing = listing[jax.random.permutation(jax.random.fold_in(own, 1), rows)]
    turn = jax.random.randint(jax.random.fold_in(own, 2), (rows, 1), 0, top)
    return jnp.take_along_axis(listing, (jnp.arange(top)[None, :] + turn) % top, axis=1)


def portions_of(number_of, total, reach, lean, full):
    portions = [(1 << 20) // math.isqrt(standing ** lean) + 1 for standing in range(1, number_of + 1)]
    largest = reach if full else min(reach, max(-(-total // number_of), total * portions[0] // sum(portions)))
    least = 1 if total - largest >= number_of - 1 else 0
    holding, surplus = [largest] + [least] * (number_of - 1), total - largest - least * (number_of - 1)
    while surplus > 0:
        movable = [i for i in range(1, number_of) if holding[i] < largest] or [i for i in range(1, number_of) if holding[i] < reach]
        pool, budget = sum([portions[i] for i in movable]), surplus
        for i in movable:
            addition = min(reach - holding[i], max(1, budget * portions[i] // pool), surplus)
            holding[i] = holding[i] + addition
            surplus = surplus - addition
    return np.array(holding)


def gaussian(rng, shape, deviation, reach, pieces=(), dtype=jnp.bfloat16):
    drawn = jax.random.normal(rng, shape, jnp.float32) * deviation
    if len(pieces) > 0:
        drawn = shard_levels(rng, shape, pieces, -0.22, 0.18) * drawn
    return jnp.clip(drawn, min=-reach, max=reach).astype(dtype)


def setup_inputs(seed: int = 0) -> dict:
    streams_of = jax.random.split(jax.random.key(seed), 11)
    hidden_states = draw_hidden_states(jax.random.fold_in(streams_of[10], 71), 0)
    dec_gain = draw_dec_gain(jax.random.fold_in(streams_of[10], 71), 0)
    nbr_tokens = draw_nbr_tokens(jax.random.fold_in(streams_of[10], 71), 0)
    enc_gain = draw_enc_gain(jax.random.fold_in(streams_of[10], 71), 0)
    query_weight = gaussian(streams_of[4], (D, H * HD), D ** -0.5, 0.09375, ((1, 8),))
    key_weight = gaussian(streams_of[5], (D, H * HD), D ** -0.5, 0.09375, ((1, 8),))
    value_weight = gaussian(streams_of[6], (D, H * HD), D ** -0.5, 0.09375, ((1, 8),))
    out_weight = gaussian(streams_of[7], (H * HD, D), (H * HD) ** -0.5, 0.09375, ((0, 8),))
    cite_owner_keys = jax.random.split(jax.random.fold_in(streams_of[8], 1), (NBRS * SPANS) // (NBRS * CH_DEV))
    cite_owner_turns = jax.random.permutation(jax.random.fold_in(streams_of[8], 3), (NBRS * SPANS) // (NBRS * CH_DEV))
    cite_owner = jax.vmap(lambda own, number: deal_out(jax.random.fold_in(streams_of[8], 2), own, number, NBRS * CH_DEV, N_DP, 1, CAP, 2))(cite_owner_keys, cite_owner_turns).reshape((NBRS * SPANS, 1))
    cite_local = set_ends(jax.random.randint(streams_of[9], (SPANS, NBRS), 0, NU_DEV), jax.random.fold_in(streams_of[9], 1), 0, NU_DEV - 1).astype(jnp.int32)
    return dict(hidden_states=hidden_states, dec_gain=dec_gain, nbr_tokens=nbr_tokens, enc_gain=enc_gain, query_weight=query_weight, key_weight=key_weight, value_weight=value_weight, out_weight=out_weight, cite_owner=cite_owner, cite_local=cite_local)


def rms_rows(rows, gain):
    values = rows.astype(jnp.float32)
    scale = lax.rsqrt(lax.optimization_barrier(jnp.mean(values * values, axis=-1, keepdims=True)) + 1e-05)
    return (values * scale * gain.astype(jnp.float32)).astype(jnp.bfloat16)

def reference(hidden_states, dec_gain, nbr_tokens, enc_gain, query_weight, key_weight, value_weight, out_weight, cite_owner, cite_local):
    kv_weight = jnp.concatenate([key_weight, value_weight], axis=1)

    def encode(tile):
        normed = rms_rows(tile, enc_gain)
        return jnp.dot(normed, kv_weight, preferred_element_type=jnp.float32).astype(jnp.bfloat16)
    encoded = lax.optimization_barrier(lax.map(encode, nbr_tokens))
    normed = rms_rows(hidden_states, dec_gain)
    queries = jnp.dot(normed, query_weight, preferred_element_type=jnp.float32).astype(jnp.bfloat16)
    queries = lax.optimization_barrier(queries)
    tile_ids = (cite_owner[:, 0].reshape(SPANS, NBRS) * NU_DEV + cite_local).astype(jnp.int32)

    def attend(inputs):
        block_q, row_ids = inputs
        kv = jnp.take(encoded, row_ids, axis=0).reshape(NBRS * NL, 2, H, HD).astype(jnp.float32)
        query_heads = block_q.reshape(SPAN, H, HD).astype(jnp.float32)
        scores = jnp.einsum('qhd,khd->hqk', query_heads, kv[:, 0]) * HD ** (-0.5)
        weights = jax.nn.softmax(scores, axis=-1).astype(jnp.bfloat16)
        weights = lax.optimization_barrier(weights).astype(jnp.float32)
        context = jnp.einsum('hqk,khd->qhd', weights, kv[:, 1]).astype(jnp.bfloat16)
        return context.reshape(SPAN, H * HD)
    context = lax.map(attend, (queries.reshape(SPANS, SPAN, H * HD), tile_ids))
    context = context.reshape(TOKENS, H * HD)
    group_width = H * HD // N_ENC
    context_groups = jnp.transpose(context.reshape(TOKENS, N_ENC, group_width), (1, 0, 2))
    weight_groups = out_weight.reshape(N_ENC, group_width, D)

    def add_group(total, inputs):
        columns, rows = inputs
        partial_value = jnp.dot(columns, rows, preferred_element_type=jnp.float32).astype(jnp.bfloat16)
        return (total + partial_value.astype(jnp.float32), None)
    total, unused = lax.scan(add_group, jnp.zeros((TOKENS, D), jnp.float32), (context_groups, weight_groups))
    return total.astype(jnp.bfloat16)
```

```python
import functools

import jax
import jax.numpy as jnp
from jax import lax
from jax.experimental import pallas as pl
from jax.experimental.pallas import tpu as pltpu
from jax.sharding import PartitionSpec as P

HD = 128
SPAN = 64
NBRS = 2
CHUNKS = 4
RS_CHUNKS = 4


def normalize(rows, gain):
    values = rows.astype(jnp.float32)
    scale = lax.rsqrt(jnp.mean(values * values, axis=-1, keepdims=True) + 1e-05)
    return (values * scale * gain.astype(jnp.float32)).astype(jnp.bfloat16)


def shift_outer(outer, inner, step):
    return [(o * inner + i, (o + step) % outer * inner + i) for o in range(outer) for i in range(inner)]


def shift_inner(outer, inner, step):
    return [(o * inner + i, o * inner + (i + step) % inner) for o in range(outer) for i in range(inner)]


def gather_slots(shard, axis, outer, inner):
    lines = [shard]
    for _ in range(outer - 1):
        lines.append(lax.ppermute(lines[-1], axis, shift_outer(outer, inner, 1)))
    slots = []
    for line in lines:
        slots.append(line)
        for _ in range(inner - 1):
            slots.append(lax.ppermute(slots[-1], axis, shift_inner(outer, inner, 1)))
    return slots


def attend_kernel(arrays, width, source_ref, place_ref, q_ref, *rest):
    kv_refs, out_ref, buf, sem = rest[:arrays], rest[arrays], rest[arrays + 1], rest[arrays + 2]
    cites = buf.shape[0]
    heads = width // HD

    def fetch(j, carry):
        for a in range(arrays):

            @pl.when(source_ref[j] == a)
            def _():
                pltpu.make_async_copy(kv_refs[a].at[place_ref[j]], buf.at[j], sem.at[j]).start()

        return carry

    lax.fori_loop(0, cites, fetch, 0)

    def span(c, carry):
        for s in range(NBRS):
            j = c * NBRS + s
            pltpu.make_async_copy(kv_refs[0].at[0], buf.at[j], sem.at[j]).wait()
        rows = pl.ds(pl.multiple_of(c * SPAN, SPAN), SPAN)
        for h in range(heads):
            q = q_ref[rows, h * HD : (h + 1) * HD]
            k = jnp.concatenate([buf[c * NBRS + s, :, h * HD : (h + 1) * HD] for s in range(NBRS)], axis=0)
            v = jnp.concatenate(
                [buf[c * NBRS + s, :, width + h * HD : width + (h + 1) * HD] for s in range(NBRS)], axis=0
            )
            scores = lax.dot_general(q, k, (((1,), (1,)), ((), ())), preferred_element_type=jnp.float32) * HD ** (-0.5)
            e = jnp.exp(scores - jnp.max(scores, axis=-1, keepdims=True))
            w = (e / jnp.sum(e, axis=-1, keepdims=True)).astype(jnp.bfloat16)
            out_ref[rows, h * HD : (h + 1) * HD] = jnp.dot(w, v, preferred_element_type=jnp.float32).astype(jnp.bfloat16)
        return carry

    lax.fori_loop(0, cites // NBRS, span, 0)


def attend(source, place, queries, pieces):
    tok_rows, width = queries.shape
    cites = source.shape[0]
    tile_len = pieces[0].shape[1]
    arrays = len(pieces)
    return pl.pallas_call(
        functools.partial(attend_kernel, arrays, width),
        out_shape=jax.ShapeDtypeStruct((tok_rows, width), jnp.bfloat16),
        in_specs=[pl.BlockSpec(memory_space=pltpu.SMEM)] * 2
        + [pl.BlockSpec(memory_space=pltpu.VMEM)]
        + [pl.BlockSpec(memory_space=pl.ANY)] * arrays,
        out_specs=pl.BlockSpec(memory_space=pltpu.VMEM),
        scratch_shapes=[
            pltpu.VMEM((cites, tile_len, 2 * width), jnp.bfloat16),
            pltpu.SemaphoreType.DMA((cites,)),
        ],
        compiler_params=pltpu.CompilerParams(vmem_limit_bytes=24 << 20),
    )(source, place, queries, *pieces)


def per_device(
    n_dp,
    n_enc,
    hidden_states,
    dec_gain,
    nbr_tokens,
    enc_gain,
    query_weight,
    key_weight,
    value_weight,
    out_weight,
    cite_owner,
    cite_local,
):
    outer = 4 if n_enc % 4 == 0 else n_enc
    inner = n_enc // outer
    cores = 2 if n_dp % 2 == 0 else 1
    chips = n_dp // cores
    me = lax.axis_index("enc")
    my_o, my_i = me // inner, me % inner
    dp_me = lax.axis_index("dp")

    kv_weight = jnp.concatenate((key_weight, value_weight), axis=1)
    tiles = nbr_tokens.shape[0]
    per_chunk = tiles // CHUNKS
    width = query_weight.shape[1]
    pieces = []
    arrived = None
    for c in range(CHUNKS):
        own = normalize(nbr_tokens[c * per_chunk : (c + 1) * per_chunk], enc_gain)
        if arrived is not None:
            own, _ = lax.optimization_barrier((own, arrived))
        slots = gather_slots(own, "enc", outer, inner)
        arrived = slots[inner]
        rows = jnp.concatenate(slots, axis=1)
        encoded = jnp.dot(rows, kv_weight, preferred_element_type=jnp.float32).astype(jnp.bfloat16)
        pieces.extend(gather_slots(encoded, "dp", chips, cores))

    hidden_own, _ = lax.optimization_barrier((hidden_states, arrived))
    slots = gather_slots(hidden_own, "enc", outer, inner)
    order = jnp.arange(n_enc)
    back = (my_o - order // inner) % outer * inner + (my_i - order % inner) % inner
    stacked = jnp.take(jnp.stack(slots), back, axis=0)
    whole = jnp.transpose(stacked, (1, 0, 2)).reshape(hidden_states.shape[0], -1)
    queries = jnp.dot(normalize(whole, dec_gain), query_weight, preferred_element_type=jnp.float32).astype(jnp.bfloat16)

    tok_rows = whole.shape[0]
    owners = cite_owner[:, 0]
    local = cite_local.reshape(-1)
    back_dp = (dp_me // cores - owners // cores) % chips * cores + (dp_me % cores - owners % cores) % cores
    source = local // per_chunk * n_dp + back_dp
    context = attend(source, local % per_chunk, queries, pieces)

    columns = out_weight.shape[1] // RS_CHUNKS
    block = tok_rows // n_enc
    outs = []
    for c in range(RS_CHUNKS):
        part = jnp.dot(
            context, out_weight[:, c * columns : (c + 1) * columns], preferred_element_type=jnp.float32
        ).astype(jnp.bfloat16)
        part = part.reshape(outer, inner, block, columns)
        total = lax.dynamic_index_in_dim(part, my_i, 1, keepdims=False).astype(jnp.float32)
        for b in range(1, inner):
            sent = lax.dynamic_index_in_dim(part, (my_i + b) % inner, 1, keepdims=False)
            total = total + lax.ppermute(sent, "enc", shift_inner(outer, inner, b)).astype(jnp.float32)
        rounded = total.astype(jnp.bfloat16)
        out = lax.dynamic_index_in_dim(total, my_o, 0, keepdims=False)
        for a in range(1, outer):
            sent = lax.dynamic_index_in_dim(rounded, (my_o + a) % outer, 0, keepdims=False)
            out = out + lax.ppermute(sent, "enc", shift_outer(outer, inner, a)).astype(jnp.float32)
        outs.append(out.astype(jnp.bfloat16))
    return jnp.concatenate(outs, axis=1)


def solution(mesh):
    in_specs = (
        P("dp", "enc"),
        P(),
        P("dp", "enc", None),
        P(),
        P(None, "enc"),
        P(None, "enc"),
        P(None, "enc"),
        P("enc", None),
        P("dp", None),
        P("dp", None),
    )
    out_specs = P(("dp", "enc"), None)
    return jax.shard_map(
        functools.partial(per_device, mesh.shape["dp"], mesh.shape["enc"]),
        mesh=mesh,
        in_specs=in_specs,
        out_specs=out_specs,
        check_vma=False,
    )
```

```python
import functools

import jax
import jax.numpy as jnp
from jax import lax
from jax.experimental import pallas as pl
from jax.experimental.pallas import tpu as pltpu
from jax.sharding import PartitionSpec as P

HD = 128
SPAN = 64
NBRS = 2
CHUNKS = 4
RS_CHUNKS = 4


def normalize(rows, gain):
    values = rows.astype(jnp.float32)
    scale = lax.rsqrt(jnp.mean(values * values, axis=-1, keepdims=True) + 1e-05)
    return (values * scale * gain.astype(jnp.float32)).astype(jnp.bfloat16)


def shift_outer(outer, inner, step):
    return [(o * inner + i, (o + step) % outer * inner + i) for o in range(outer) for i in range(inner)]


def shift_inner(outer, inner, step):
    return [(o * inner + i, o * inner + (i + step) % inner) for o in range(outer) for i in range(inner)]


def gather_slots(shard, axis, outer, inner):
    lines = [shard]
    for _ in range(outer - 1):
        lines.append(lax.ppermute(lines[-1], axis, shift_outer(outer, inner, 1)))
    slots = []
    for line in lines:
        slots.append(line)
        for _ in range(inner - 1):
            slots.append(lax.ppermute(slots[-1], axis, shift_inner(outer, inner, 1)))
    return slots


def gather_any_order(shard, axis, outer, inner):
    slots = [shard]
    for _ in range(inner - 1):
        slots.append(lax.ppermute(slots[-1], axis, shift_inner(outer, inner, 1)))
    for start in range(inner):
        line = slots[start]
        for _ in range(outer - 1):
            line = lax.ppermute(line, axis, shift_outer(outer, inner, 1))
            slots.append(line)
    return slots


def attend_kernel(arrays, width, source_ref, place_ref, q_ref, *rest):
    kv_refs, out_ref, buf, sem = rest[:arrays], rest[arrays], rest[arrays + 1], rest[arrays + 2]
    cites = buf.shape[0]
    heads = width // HD

    def fetch(j, carry):
        for a in range(arrays):

            @pl.when(source_ref[j] == a)
            def _():
                pltpu.make_async_copy(kv_refs[a].at[place_ref[j]], buf.at[j], sem.at[j]).start()

        return carry

    lax.fori_loop(0, cites, fetch, 0)

    def span(c, carry):
        for s in range(NBRS):
            j = c * NBRS + s
            pltpu.make_async_copy(kv_refs[0].at[0], buf.at[j], sem.at[j]).wait()
        rows = pl.ds(pl.multiple_of(c * SPAN, SPAN), SPAN)
        for h in range(heads):
            q = q_ref[rows, h * HD : (h + 1) * HD]
            k = jnp.concatenate([buf[c * NBRS + s, :, h * HD : (h + 1) * HD] for s in range(NBRS)], axis=0)
            v = jnp.concatenate(
                [buf[c * NBRS + s, :, width + h * HD : width + (h + 1) * HD] for s in range(NBRS)], axis=0
            )
            scores = lax.dot_general(q, k, (((1,), (1,)), ((), ())), preferred_element_type=jnp.float32) * HD ** (-0.5)
            e = jnp.exp(scores - jnp.max(scores, axis=-1, keepdims=True))
            w = (e / jnp.sum(e, axis=-1, keepdims=True)).astype(jnp.bfloat16)
            out_ref[rows, h * HD : (h + 1) * HD] = jnp.dot(w, v, preferred_element_type=jnp.float32).astype(jnp.bfloat16)
        return carry

    lax.fori_loop(0, cites // NBRS, span, 0)


def attend(source, place, queries, pieces):
    tok_rows, width = queries.shape
    cites = source.shape[0]
    tile_len = pieces[0].shape[1]
    arrays = len(pieces)
    return pl.pallas_call(
        functools.partial(attend_kernel, arrays, width),
        out_shape=jax.ShapeDtypeStruct((tok_rows, width), jnp.bfloat16),
        in_specs=[pl.BlockSpec(memory_space=pltpu.SMEM)] * 2
        + [pl.BlockSpec(memory_space=pltpu.VMEM)]
        + [pl.BlockSpec(memory_space=pl.ANY)] * arrays,
        out_specs=pl.BlockSpec(memory_space=pltpu.VMEM),
        scratch_shapes=[
            pltpu.VMEM((cites, tile_len, 2 * width), jnp.bfloat16),
            pltpu.SemaphoreType.DMA((cites,)),
        ],
        compiler_params=pltpu.CompilerParams(vmem_limit_bytes=24 << 20),
    )(source, place, queries, *pieces)


def per_device(
    n_dp,
    n_enc,
    hidden_states,
    dec_gain,
    nbr_tokens,
    enc_gain,
    query_weight,
    key_weight,
    value_weight,
    out_weight,
    cite_owner,
    cite_local,
):
    outer = 4 if n_enc % 4 == 0 else n_enc
    inner = n_enc // outer
    cores = 2 if n_dp % 2 == 0 else 1
    chips = n_dp // cores
    me = lax.axis_index("enc")
    my_o, my_i = me // inner, me % inner
    dp_me = lax.axis_index("dp")

    kv_weight = jnp.concatenate((key_weight, value_weight), axis=1)
    tiles = nbr_tokens.shape[0]
    per_chunk = tiles // CHUNKS
    width = query_weight.shape[1]
    pieces = []
    arrived = None
    for c in range(CHUNKS):
        own = normalize(nbr_tokens[c * per_chunk : (c + 1) * per_chunk], enc_gain)
        if arrived is not None:
            own, _ = lax.optimization_barrier((own, arrived))
        inner_first = c == CHUNKS // 2
        slots = (gather_any_order if inner_first else gather_slots)(own, "enc", outer, inner)
        arrived = slots[inner]
        rows = jnp.concatenate(slots, axis=1)
        encoded = jnp.dot(rows, kv_weight, preferred_element_type=jnp.float32).astype(jnp.bfloat16)
        pieces.extend(gather_slots(encoded, "dp", chips, cores))

    hidden_own, _ = lax.optimization_barrier((hidden_states, arrived))
    slots = gather_slots(hidden_own, "enc", outer, inner)
    order = jnp.arange(n_enc)
    back = (my_o - order // inner) % outer * inner + (my_i - order % inner) % inner
    part_len = hidden_states.shape[1]
    weight_rows = jnp.take(query_weight.reshape(n_enc, part_len, width), back, axis=0).reshape(-1, width)
    gain = jnp.take(dec_gain.reshape(n_enc, part_len), back, axis=0).reshape(-1)
    whole = jnp.concatenate(slots, axis=1)
    queries = jnp.dot(normalize(whole, gain), weight_rows, preferred_element_type=jnp.float32).astype(jnp.bfloat16)

    tok_rows = whole.shape[0]
    owners = cite_owner[:, 0]
    local = cite_local.reshape(-1)
    back_dp = (dp_me // cores - owners // cores) % chips * cores + (dp_me % cores - owners % cores) % cores
    source = local // per_chunk * n_dp + back_dp
    context = attend(source, local % per_chunk, queries, pieces)

    columns = out_weight.shape[1] // RS_CHUNKS
    block = tok_rows // n_enc
    outs = []
    for c in range(RS_CHUNKS):
        part = jnp.dot(
            context, out_weight[:, c * columns : (c + 1) * columns], preferred_element_type=jnp.float32
        ).astype(jnp.bfloat16)
        part = part.reshape(outer, inner, block, columns)
        total = lax.dynamic_index_in_dim(part, my_i, 1, keepdims=False).astype(jnp.float32)
        for b in range(1, inner):
            sent = lax.dynamic_index_in_dim(part, (my_i + b) % inner, 1, keepdims=False)
            total = total + lax.ppermute(sent, "enc", shift_inner(outer, inner, b)).astype(jnp.float32)
        rounded = total.astype(jnp.bfloat16)
        out = lax.dynamic_index_in_dim(total, my_o, 0, keepdims=False)
        for a in range(1, outer):
            sent = lax.dynamic_index_in_dim(rounded, (my_o + a) % outer, 0, keepdims=False)
            out = out + lax.ppermute(sent, "enc", shift_outer(outer, inner, a)).astype(jnp.float32)
        outs.append(out.astype(jnp.bfloat16))
    return jnp.concatenate(outs, axis=1)


def solution(mesh):
    in_specs = (
        P("dp", "enc"),
        P(),
        P("dp", "enc", None),
        P(),
        P(None, "enc"),
        P(None, "enc"),
        P(None, "enc"),
        P("enc", None),
        P("dp", None),
        P("dp", None),
    )
    out_specs = P(("dp", "enc"), None)
    return jax.shard_map(
        functools.partial(per_device, mesh.shape["dp"], mesh.shape["enc"]),
        mesh=mesh,
        in_specs=in_specs,
        out_specs=out_specs,
        check_vma=False,
    )
```
